128 devices in a mesh: row: 8 (over z, core), col: 16 (over y, x).
Axes of the slice: x: 4, y: 4, z: 4, core: 2. Of those that a mesh axis runs over, the one named last changes fastest.
Arguments:
- fock: bfloat16 [18432, 18432], P('row', 'col'), may hold values from -6 to 6
- intersection: bfloat16 [18432, 18432], P('row', 'col'), may hold values from -6 to 6
- tile_mask: int32 [2, 144, 144], P(None, 'row', 'col'), may hold values 0 or 1
- coefficients: bfloat16 [256, 7, 20, 128], P(('row', 'col')), may hold values from -0.5 to 0.5
- domains: int32 [256, 7], P(('row', 'col')), may hold values from 0 to 143, all different within a row; in each aligned block of 32 rows (0 to 31, 32 to 63, ...) at most 2 rows name the same one
- neighbours: int32 [256, 2], P(('row', 'col')), may hold values from 0 to 255, all different within a row
- amplitudes: float32 [256, 20, 20], P(('row', 'col')), may hold values from -0.18 to 0.18
Outputs:
- projected: float32 [256, 20, 20], P(('row', 'col'))
The draws below stay inside these ranges and needn't reach their ends.
Inputs may be any that keep to these rules, and one draw needn't show every extreme that they name: `domains`: each pair names 7 different tiles; among the 32 pairs of one row index (an aligned block of pairs) no tile is named by more than 2 slots. `neighbours`: each pair names 2 different pairs.
All inputs are finite; a program needn't handle non-finite values. No bound on the sum of `tile_mask` on one device may be relied on, other than what follows from the above.
Results may differ from the reference program's by a relative error of at most 0.0041.
Values may be sent and summed in bfloat16 or wider, within the bound.
A program may use at most 256 MiB of HBM per device.

```python
import math
import jax
import jax.numpy as jnp
import numpy as np
from jax import lax

NT = 144
TILE = 128
NPNO = 20
DT = 7
NB = 2
MOST = 2
GROUP = 32
PAIRS = 256
NPAO = 18432
N_ROW = 8


def set_ends(result, stream_key, smallest, top_value):
    longest = result.shape.index(max(result.shape))
    spots = []
    for shift in (0, 1):
        where = [jax.random.randint(jax.random.fold_in(stream_key, axis), (), 0, length) for axis, length in enumerate(result.shape)]
        where[longest] = (where[longest] + shift) % result.shape[longest]
        spots.append(tuple(where))
    return result.at[spots[0]].set(smallest).at[spots[1]].set(top_value)


def block_levels(stream_key, shape, shards, smallest, largest):
    def one(dim, blocks):
        heights = jax.random.uniform(jax.random.fold_in(jax.random.fold_in(stream_key, 6), dim), (blocks,), jnp.float32, smallest / len(shards), largest / len(shards))
        return jnp.repeat(jnp.exp(heights), shape[dim] // blocks).reshape((-1,) + (1,) * (len(shape) - dim - 1))

    loudness = one(*shards[0])
    for cut in shards[1:]:
        loudness = loudness * one(*cut)
    return loudness


def choose_distinct(key, rows, count, top, lift):
    order = jax.random.permutation(jax.random.fold_in(key, 1), count)
    favour = order
    for power in range(3):
        favour = favour * favour // count
    favour = favour * lift // count
    lots = jax.random.randint(jax.random.fold_in(key, 2), (rows, count), 0, 4096) + favour
    sure = jax.random.permutation(jax.random.fold_in(key, 3), rows)[jnp.arange(count) % rows]
    lots = jnp.where(jnp.arange(rows)[:, None] == sure[None, :], 1 << 14, lots)
    score = lots * count + jnp.arange(count)
    return lax.top_k(score.astype(jnp.int32), top)[1].astype(jnp.int32)


def assign_block(key, own, number, rows, amount, top, most, lean):
    ranking = jax.random.permutation(key, amount)
    packed, usual = load_shares(amount, rows * top, most, lean, True), load_shares(amount, rows * top, most, lean, False)
    places = jnp.arange(amount)

    def named(lengths, offset_by):
        used = int((lengths > 0).sum())
        fixed = max(1, used // 4)
        moved = fixed + (places - fixed + offset_by * (used - fixed)) % max(1, amount - fixed)
        return jnp.zeros((amount,), jnp.int32).at[ranking[jnp.where(places < fixed, places, moved)]].set(jnp.asarray(lengths, jnp.int32))

    lengths = jnp.where(number % 4 == 0, named(packed, number // 4), named(usual, number - number // 4 - 1))
    mixed = jax.random.permutation(jax.random.fold_in(own, 3), amount)
    giver, taker = mixed[0:amount // 2 * 2:2], mixed[1:amount // 2 * 2:2]
    margin = jnp.minimum(lengths[giver] - 1, most - lengths[taker]) // 2
    margin = jnp.where((giver == ranking[0]) | (taker == ranking[0]) | (lengths[taker] == 0), 0, jnp.maximum(margin, 0))
    moved = jax.random.randint(jax.random.fold_in(own, 4), (amount // 2,), 0, 1 << 20) % (margin + 1)
    lengths = lengths.at[giver].add(-moved).at[taker].add(moved)
    labels = jnp.searchsorted(jnp.cumsum(lengths), jnp.arange(rows * top), side="right").astype(jnp.int32)
    table = labels.reshape(top, rows).T
    table = table[jax.random.permutation(jax.random.fold_in(own, 1), rows)]
    offset_by = jax.random.randint(jax.random.fold_in(own, 2), (rows, 1), 0, top)
    return jnp.take_along_axis(table, (jnp.arange(top)[None, :] + offset_by) % top, axis=1)


def load_shares(number_of, total, reach, lean, full):
    weights = [(1 << 20) // math.isqrt(rank ** lean) + 1 for rank in range(1, number_of + 1)]
    largest = reach if full else min(reach, max(-(-total // number_of), total * weights[0] // sum(weights)))
    least = 1 if total - largest >= number_of - 1 else 0
    given, rest = [largest] + [least] * (number_of - 1), total - largest - least * (number_of - 1)
    while rest > 0:
        movable = [i for i in range(1, number_of) if given[i] < largest] or [i for i in range(1, number_of) if given[i] < reach]
        mass, budget = sum([weights[i] for i in movable]), rest
        for i in movable:
            more = min(reach - given[i], max(1, budget * weights[i] // mass), rest)
            given[i] = given[i] + more
            rest = rest - more
    return np.array(given)


def centred(own_key, dims, scale, limit, split=(), kind=jnp.bfloat16):
    entries = jax.random.normal(own_key, dims, jnp.float32) * scale
    if len(split) > 0:
        entries = block_levels(own_key, dims, split, -0.22, 0.18) * entries
    return jnp.clip(entries, min=-limit, max=limit).astype(kind)


def setup_inputs(seed: int = 0) -> dict:
    seeds = jax.random.split(jax.random.key(seed), 8)
    fock = centred(seeds[0], (NPAO, NPAO), 1.0, 6.0, ((0, 8), (1, 16)))
    intersection = centred(seeds[1], (NPAO, NPAO), 1.0, 6.0, ((0, 8), (1, 16)))
    tile_mask = set_ends((jax.random.randint(seeds[2], (2, NT, NT), 0, 2) < 1).astype(jnp.int32), jax.random.fold_in(seeds[2], 1), 0, 1)
    coefficients = centred(seeds[3], (PAIRS, DT, NPNO, TILE), TILE ** -0.5, 0.5, ((0, 128),))
    domains_keys = jax.random.split(jax.random.fold_in(seeds[4], 1), PAIRS // GROUP)
    domains_turns = jax.random.permutation(jax.random.fold_in(seeds[4], 3), PAIRS // GROUP)
    domains = jax.vmap(lambda own, number: assign_block(jax.random.fold_in(seeds[4], 2), own, number, GROUP, NT, DT, MOST, 2))(domains_keys, domains_turns).reshape((PAIRS, DT))
    neighbours = choose_distinct(seeds[5], PAIRS, PAIRS, NB, 64)
    amplitudes = centred(seeds[6], (PAIRS, NPNO, NPNO), 0.03, 0.18, ((0, 128),), jnp.float32)
    return dict(fock=fock, intersection=intersection, tile_mask=tile_mask, coefficients=coefficients, domains=domains, neighbours=neighbours, amplitudes=amplitudes)


HIGH = lax.Precision.HIGHEST


def reference(fock, intersection, tile_mask, coefficients, domains, neighbours, amplitudes):
    tile_rows = NT // N_ROW
    fock_tiles = fock.reshape(NT, TILE, NT, TILE)
    over_tiles = intersection.reshape(NT, TILE, NT, TILE)
    group_ids = jnp.arange(N_ROW).astype(jnp.int32)

    def one_pair(inputs):
        own_coeffs, own_tiles, own_links = inputs
        link_tiles = jnp.take(domains, own_links, axis=0)
        link_coeffs = jnp.take(coefficients, own_links, axis=0)
        rows_index = own_tiles[:, None, None]
        cols_index = link_tiles[None, :, :]
        fock_blocks = fock_tiles[rows_index, :, cols_index, :]
        fock_blocks = fock_blocks * tile_mask[0][rows_index, cols_index].astype(jnp.bfloat16)[..., None, None]
        over_blocks = over_tiles[rows_index, :, cols_index, :]
        over_blocks = over_blocks * tile_mask[1][rows_index, cols_index].astype(jnp.bfloat16)[..., None, None]
        blocks = jnp.stack([fock_blocks, over_blocks], axis=3).astype(jnp.float32)
        parts = jnp.einsum("sak,snumkv->sanumv", own_coeffs.astype(jnp.float32), blocks, precision=HIGH)
        onehot = (group_ids[:, None] == (own_tiles // tile_rows)[None, :]).astype(jnp.float32)
        partial_sum = jnp.einsum("rs,sanumv->ranumv", onehot, parts, precision=HIGH).astype(jnp.bfloat16)
        partial_sum = lax.optimization_barrier(partial_sum).astype(jnp.float32)
        cross = jnp.einsum("ranumv,nubv->nmab", partial_sum, link_coeffs.astype(jnp.float32), precision=HIGH)
        nearby = jnp.take(amplitudes, own_links, axis=0)
        fock_part = cross[:, 0]
        over_part = cross[:, 1]
        first = jnp.einsum("nab,nbc,ndc->ad", over_part, nearby, fock_part, precision=HIGH)
        second = jnp.einsum("nab,nbc,ndc->ad", fock_part, nearby, over_part, precision=HIGH)
        return first + second

    return lax.map(one_pair, (coefficients, domains, neighbours))
```

```python
import functools
import jax
import jax.numpy as jnp
from jax import lax
from jax.experimental import pallas as pl
from jax.experimental.pallas import tpu as pltpu
from jax.sharding import PartitionSpec as P

HIGH = lax.Precision.HIGHEST
UNROLL = 4
LANES = 32


def slot_tables(tiles, first, count):
    packed = jnp.zeros(tiles.shape[:1], jnp.int32)
    seen = jnp.zeros(tiles.shape[:1], jnp.int32)
    for s in range(tiles.shape[1]):
        here = ((tiles[:, s] >= first) & (tiles[:, s] < first + count)).astype(jnp.int32)
        packed = packed + here * (s << (3 * seen))
        seen = seen + here
    return packed, seen


def pair_blocks_kernel(
    dims, dom, nb, rowp, colp, work, mask, c_hbm, f_hbm, s_hbm, g_ref, cv, fv, sv, l1, l2, sems
):
    pairs, slots, rows, tile, tile_rows, tile_cols = dims
    copies = (
        pltpu.make_async_copy(c_hbm, cv, sems.at[0]),
        pltpu.make_async_copy(f_hbm, fv, sems.at[1]),
        pltpu.make_async_copy(s_hbm, sv, sems.at[2]),
    )
    for c in copies:
        c.start()
    row0 = lax.axis_index("row") * tile_rows
    col0 = lax.axis_index("col") * tile_cols
    g_ref[...] = jnp.zeros_like(g_ref)
    cells = tile_rows * tile_cols

    def one_pair(d, i, counts):
        p = 2 * d + i
        w = work[p]

        def busy(counts):
            out = list(counts)
            packed_rows = rowp[p]
            n_rows = w & 7
            for n in range(2):
                q = 2 * i + n
                k = nb[2 * p + n]
                packed_cols = colp[k]
                n_cols = (w >> (3 + 3 * n)) & 7

                def by_row(x, cnt, k=k, packed_cols=packed_cols, n_cols=n_cols, q=q):
                    sa = p * slots + ((packed_rows >> (3 * x)) & 7)
                    a = dom[sa] - row0

                    def by_col(y, cnt):
                        sb = k * slots + ((packed_cols >> (3 * y)) & 7)
                        b = dom[sb] - col0
                        cell = a * tile_cols + b
                        m0 = mask[cell]
                        m1 = mask[cells + cell]
                        l1[q, cnt] = sa | (sb << 11) | (a << 22) | (b << 27)
                        l2[q, cnt] = d | (m0 << 8) | (m1 << 9)
                        return cnt + (m0 | m1)

                    return lax.fori_loop(0, n_cols, by_col, cnt)

                out[q] = lax.fori_loop(0, n_rows, by_row, out[q])
            return tuple(out)

        return lax.cond(w != 0, busy, lambda c: c, counts)

    def per_device(d, counts):
        counts = one_pair(d, 0, counts)
        return one_pair(d, 1, counts)

    zero = jnp.int32(0)
    counts = lax.fori_loop(0, pairs // 2, per_device, (zero, zero, zero, zero))
    for q in range(4):
        for x in range(UNROLL):
            l1[q, counts[q] + x] = zero
            l2[q, counts[q] + x] = zero
    for c in copies:
        c.wait()

    def product(q, i):
        w1 = l1[q, i]
        w2 = l2[q, i]
        sa = w1 & 2047
        sb = (w1 >> 11) & 2047
        a = pl.multiple_of(((w1 >> 22) & 31) * tile, tile)
        b = pl.multiple_of(((w1 >> 27) & 15) * tile, tile)
        both = jnp.concatenate([fv[pl.ds(a, tile), pl.ds(b, tile)], sv[pl.ds(a, tile), pl.ds(b, tile)]], axis=1)
        t = jnp.dot(cv[sa], both, preferred_element_type=jnp.float32)
        m0 = ((w2 >> 8) & 1).astype(jnp.float32)
        m1 = ((w2 >> 9) & 1).astype(jnp.float32)
        partner = cv[sb]
        dn = (((1,), (1,)), ((), ()))
        uf = lax.dot_general((t[:, :tile] * m0).astype(jnp.bfloat16), partner, dn, preferred_element_type=jnp.float32)
        us = lax.dot_general((t[:, tile:] * m1).astype(jnp.bfloat16), partner, dn, preferred_element_type=jnp.float32)
        return w2 & 255, uf, us

    for q in range(4):
        lo = q * LANES

        def body(it, carry, q=q, lo=lo):
            done = [product(q, it * UNROLL + x) for x in range(UNROLL)]
            for d, uf, us in done:
                g_ref[2 * d, :rows, lo : lo + rows] += uf
                g_ref[2 * d + 1, :rows, lo : lo + rows] += us
            return carry

        lax.fori_loop(0, (counts[q] + UNROLL - 1) // UNROLL, body, 0)


def shards(fock, intersection, tile_mask, coefficients, domains, neighbours, amplitudes):
    pair_dev, slots, rows, tile = coefficients.shape
    tile_rows, tile_cols = fock.shape[0] // tile, fock.shape[1] // tile
    n_dev = lax.axis_size("row") * lax.axis_size("col")
    pairs = pair_dev * n_dev
    both = ("row", "col")
    c_all = lax.all_gather(coefficients.reshape(pair_dev * slots, rows, tile), both, axis=0, tiled=True)
    tabs = lax.all_gather(jnp.concatenate([domains, neighbours], axis=1), both, axis=0, tiled=True)
    dom, nb = tabs[:, :slots], tabs[:, slots:]
    rowp, rown = slot_tables(dom, lax.axis_index("row") * tile_rows, tile_rows)
    colp, coln = slot_tables(dom, lax.axis_index("col") * tile_cols, tile_cols)
    linked = jnp.take(coln, nb.reshape(-1), axis=0).reshape(pairs, 2)
    work = rown | (linked[:, 0] << 3) | (linked[:, 1] << 6)
    work = jnp.where((rown > 0) & (linked.sum(axis=1) > 0), work, 0)
    smem = pl.BlockSpec(memory_space=pltpu.SMEM)
    anys = pl.BlockSpec(memory_space=pl.ANY)
    cap = tile_rows * 2 * (pairs // 32) // 2 * slots + 2 * UNROLL
    g = pl.pallas_call(
        functools.partial(pair_blocks_kernel, (pairs, slots, rows, tile, tile_rows, tile_cols)),
        out_shape=jax.ShapeDtypeStruct((2 * n_dev, 24, 128), jnp.float32),
        in_specs=[smem] * 6 + [anys] * 3,
        out_specs=pl.BlockSpec(memory_space=pltpu.VMEM),
        scratch_shapes=[
            pltpu.VMEM((pairs * slots, rows, tile), jnp.bfloat16),
            pltpu.VMEM(fock.shape, jnp.bfloat16),
            pltpu.VMEM(fock.shape, jnp.bfloat16),
            pltpu.SMEM((4, 2048), jnp.int32),
            pltpu.SMEM((4, 2048), jnp.int32),
            pltpu.SemaphoreType.DMA((3,)),
        ],
        compiler_params=pltpu.CompilerParams(vmem_limit_bytes=56 * 2**20),
    )(dom.reshape(-1), nb.reshape(-1), rowp, colp, work, tile_mask.reshape(-1), c_all, fock, intersection)
    g = g.reshape(lax.axis_size("row"), lax.axis_size("col"), 2, 24, 128)
    g = lax.all_to_all(g, "col", split_axis=1, concat_axis=1, tiled=True).sum(axis=1)
    g = lax.all_to_all(g, "row", split_axis=0, concat_axis=0, tiled=True).sum(axis=0)
    blocks = g[:, :rows].reshape(2, rows, 2, 2, LANES)[..., :rows]
    fock_part = jnp.transpose(blocks[0], (1, 2, 0, 3))
    over_part = jnp.transpose(blocks[1], (1, 2, 0, 3))
    every_amp = lax.all_gather(amplitudes, both, axis=0, tiled=True)
    nearby = jnp.take(every_amp, neighbours, axis=0)
    first = jnp.einsum("pnab,pnbc,pndc->pad", over_part, nearby, fock_part, precision=HIGH)
    second = jnp.einsum("pnab,pnbc,pndc->pad", fock_part, nearby, over_part, precision=HIGH)
    return first + second


def solution(mesh):
    placed = (
        P("row", "col"),
        P("row", "col"),
        P(None, "row", "col"),
        P(("row", "col"), None, None, None),
        P(("row", "col"), None),
        P(("row", "col"), None),
        P(("row", "col"), None, None),
    )
    return jax.shard_map(
        shards, mesh=mesh, in_specs=placed, out_specs=P(("row", "col"), None, None), check_vma=False
    )
```

```python
import functools
import jax
import jax.numpy as jnp
import numpy as np
from jax import lax
from jax.experimental import pallas as pl
from jax.experimental.pallas import tpu as pltpu
from jax.sharding import PartitionSpec as P

HIGH = lax.Precision.HIGHEST
UNROLL = 4
LANES = 32
MESH = pl.DeviceIdType.MESH
SIDE = 4
SHARES = ((0, 5), (5, 5), (10, 4))
ORDERS = ("xyz", "yzx", "zxy")


def chip_place():
    row, col = lax.axis_index("row"), lax.axis_index("col")
    return {"z": lax.div(row, 2), "y": lax.div(col, SIDE), "x": lax.rem(col, SIDE)}, lax.rem(row, 2)


def device_at(place, core):
    return (place["z"] * 2 + core, place["y"] * SIDE + place["x"])


def moved(place, axis, step):
    return {**place, axis: lax.rem(place[axis] + step + SIDE, SIDE)}


def slot_address(pairs, slots):
    p, s = np.divmod(np.arange(pairs * slots), slots)
    device, within = p // 2, (p % 2) * slots + s
    row, col = device // 16, device % 16
    at = {"z": row // 2, "y": col // SIDE, "x": col % SIDE}
    out = np.zeros(pairs * slots, np.int32)
    for (first, count), order in zip(SHARES, ORDERS):
        a, b, c = (at[axis] for axis in order)
        place = (((row % 2) * SIDE + c) * SIDE + b) * SIDE + a
        mine = (within >= first) & (within < first + count)
        out[mine] = (first * (pairs // 2) + place * count + within - first)[mine]
    return out


def gather_kernel(own, meta, o0, o1, o2, om, send, recv, local):
    place, core = chip_place()
    barrier = pltpu.get_barrier_semaphore()
    peers = [device_at(moved(place, axis, step), core) for axis in "xyz" for step in (1, -1)]
    peers.append(device_at(place, 1 - core))
    for peer in peers:
        pl.semaphore_signal(barrier, inc=1, device_id=peer, device_id_type=MESH)
    pl.semaphore_wait(barrier, len(peers))
    started = []

    def push(src, dst, peer):
        i = len(started)
        copy = pltpu.make_async_remote_copy(
            src_ref=src, dst_ref=dst, send_sem=send.at[i], recv_sem=recv.at[i], device_id=peer, device_id_type=MESH
        )
        copy.start()
        started.append(copy)
        return copy

    def index(axis, step):
        return lax.rem(place[axis] + step + SIDE, SIDE)

    plans = []
    for k, (out, order) in enumerate(zip((o0, o1, o2, om), ORDERS + ORDERS[2:])):
        if k < 3:
            src = own.at[pl.ds(*SHARES[k])]
            half = SHARES[k][1] // 2
            parts = (pl.ds(0, half), pl.ds(half, SHARES[k][1] - half))
        else:
            src, parts = meta, (None, None)
        plans.append((k, out.at[core], out, order, src, parts))

    keep, state = [], [dict() for _ in plans]
    for k, out, _, (a, b, c), src, _ in plans:
        here = out.at[index(c, 0), index(b, 0), index(a, 0)]
        state[k]["a"] = [push(src, here, device_at(moved(place, a, step), core)) for step in (1, -1)]
        copy = pltpu.make_async_copy(src, here, local.at[k])
        copy.start()
        keep.append(copy)
    for k, out, _, (a, b, c), _, parts in plans:
        later = []
        for step, copy, part in zip((1, -1), state[k]["a"], parts):
            copy.wait_recv()
            if part is None:
                if step == 1:
                    block = out.at[index(c, 0), index(b, 0), index(a, -1)]
                    later.append(push(block, block, device_at(moved(place, a, 1), core)))
                continue
            block = out.at[index(c, 0), index(b, 0), index(a, -step), part]
            later.append(push(block, block, device_at(moved(place, a, step), core)))
        state[k]["aa"] = later

    def line(out, axes, j):
        return out.at[index(axes[2], 0), index(axes[1], j)]

    def spread(k, j):
        _, out, _, axes, _, _ = plans[k]
        block = line(out, axes, j)
        state[k]["c%d" % j] = [push(block, block, device_at(moved(place, axes[2], step), core)) for step in (1, -1)]

    def pass_on(k, j):
        _, out, _, (a, b, c), _, _ = plans[k]
        later = []
        for step, copy in zip((1, -1), state[k]["c%d" % j]):
            copy.wait_recv()
            part = pl.ds(0, 2) if step == 1 else pl.ds(2, 2)
            block = out.at[index(c, -step), index(b, j), part]
            later.append(push(block, block, device_at(moved(place, c, step), core)))
        state[k]["cc%d" % j] = later

    def share(k, step):
        _, out, _, (a, b, c), _, _ = plans[k]
        block = out.at[index(c, step)]
        state[k].setdefault("share", []).append(push(block, block, device_at(place, 1 - core)))

    for k, out, _, (a, b, c), _, _ in plans:
        for copy in state[k]["aa"]:
            copy.wait_recv()
        keep[k].wait()
        block = line(out, (a, b, c), 0)
        state[k]["b"] = [push(block, block, device_at(moved(place, b, step), core)) for step in (1, -1)]
        spread(k, 0)
    for k, out, _, (a, b, c), _, _ in plans:
        later = []
        for step, copy in zip((1, -1), state[k]["b"]):
            copy.wait_recv()
            part = pl.ds(0, 2) if step == 1 else pl.ds(2, 2)
            block = out.at[index(c, 0), index(b, -step), part]
            later.append(push(block, block, device_at(moved(place, b, step), core)))
            spread(k, -step)
        state[k]["bb"] = later
    for k in range(4):
        pass_on(k, 0)
    for k in range(4):
        for copy in state[k]["bb"]:
            copy.wait_recv()
        spread(k, 2)
        share(k, 0)
    for j in (-1, 1, 2):
        for k in range(4):
            pass_on(k, j)
    for k in range(4):
        share(k, -1)
        share(k, 1)
    for k in range(4):
        for j in (0, -1, 1, 2):
            for copy in state[k]["cc%d" % j]:
                copy.wait_recv()
        share(k, 2)
    for k in range(4):
        for copy in state[k]["share"]:
            copy.wait_recv()
    for copy in started:
        copy.wait_send()


def gather_all(coefficients, meta):
    count, rows, tile = coefficients.shape
    cube = (2, SIDE, SIDE, SIDE)
    shapes = [jax.ShapeDtypeStruct(cube + (n, rows, tile), coefficients.dtype) for _, n in SHARES]
    shapes.append(jax.ShapeDtypeStruct(cube + meta.shape, meta.dtype))
    copies = 3 * 28 + 27
    return pl.pallas_call(
        gather_kernel,
        name="gather",
        out_shape=shapes,
        in_specs=[pl.BlockSpec(memory_space=pltpu.VMEM)] * 2,
        out_specs=[pl.BlockSpec(memory_space=pl.ANY)] * 4,
        scratch_shapes=[
            pltpu.SemaphoreType.DMA((copies,)),
            pltpu.SemaphoreType.DMA((copies,)),
            pltpu.SemaphoreType.DMA((4,)),
        ],
        compiler_params=pltpu.CompilerParams(collective_id=0, has_side_effects=True),
    )(coefficients, meta)


def reduce_kernel(g, out, other, mine, arrived, sems, send, recv):
    place, core = chip_place()
    steps = [(dz, dy, dx) for dz in range(SIDE) for dy in range(SIDE) for dx in range(SIDE)]
    barrier = pltpu.get_barrier_semaphore()
    partner = device_at(place, 1 - core)

    def chip(dz, dy, dx):
        return moved(moved(moved(place, "z", dz), "y", dy), "x", dx)

    def blocks_of(at):
        return pl.ds(2 * ((at["z"] * SIDE + at["y"]) * SIDE + at["x"]), 2)

    peers = [device_at(chip(*d), core) for d in steps[1:]] + [partner]
    for peer in peers:
        pl.semaphore_signal(barrier, inc=1, device_id=peer, device_id_type=MESH)
    pl.semaphore_wait(barrier, len(peers))
    plane = 2 * SIDE * SIDE
    swaps = []
    for d in range(SIDE):
        part = pl.ds(lax.rem(place["z"] + d + 1, SIDE) * plane, plane)
        swaps.append(
            pltpu.make_async_remote_copy(
                src_ref=g.at[1 - core, part], dst_ref=other.at[part], send_sem=sems.at[0, d],
                recv_sem=sems.at[1, d], device_id=partner, device_id_type=MESH,
            )
        )
        swaps[-1].start()
    copies = []
    for d in range(SIDE):
        swaps[d].wait_recv()
        part = pl.ds(lax.rem(place["z"] + d + 1, SIDE) * plane, plane)
        mine[part] = (g[core, part] + other[part]).astype(mine.dtype)
        for i, step in enumerate(steps):
            if step[0] == (d + 1) % SIDE and i > 0:
                at = chip(*step)
                copy = pltpu.make_async_remote_copy(
                    src_ref=mine.at[blocks_of(at)], dst_ref=arrived.at[i], send_sem=send.at[i],
                    recv_sem=recv.at[i], device_id=device_at(at, core), device_id_type=MESH,
                )
                copy.start()
                copies.append((i, copy))
    own = blocks_of(place)
    total = g[core, own] + other[own]
    for i, copy in copies:
        copy.wait_recv()
        total = total + arrived[i].astype(jnp.float32)
    out[...] = total
    for copy in swaps:
        copy.wait_send()
    for _, copy in copies:
        copy.wait_send()


def reduce_all(g):
    _, blocks, rows, lanes = g.shape
    chips = blocks // 2
    vmem = pl.BlockSpec(memory_space=pltpu.VMEM)
    return pl.pallas_call(
        reduce_kernel,
        name="reduce",
        out_shape=jax.ShapeDtypeStruct((2, rows, lanes), jnp.float32),
        in_specs=[vmem],
        out_specs=vmem,
        scratch_shapes=[
            pltpu.VMEM((blocks, rows, lanes), jnp.float32),
            pltpu.VMEM((blocks, rows, lanes), jnp.bfloat16),
            pltpu.VMEM((chips, 2, rows, lanes), jnp.bfloat16),
            pltpu.SemaphoreType.DMA((2, SIDE)),
            pltpu.SemaphoreType.DMA((chips,)),
            pltpu.SemaphoreType.DMA((chips,)),
        ],
        compiler_params=pltpu.CompilerParams(collective_id=1, has_side_effects=True, vmem_limit_bytes=40 * 2**20),
    )(g)


def slot_tables(tiles, first, count):
    packed = jnp.zeros(tiles.shape[:1], jnp.int32)
    seen = jnp.zeros(tiles.shape[:1], jnp.int32)
    for s in range(tiles.shape[1]):
        here = ((tiles[:, s] >= first) & (tiles[:, s] < first + count)).astype(jnp.int32)
        packed = packed + here * (s << (3 * seen))
        seen = seen + here
    return packed, seen


def pair_blocks_kernel(
    dims, dom, address, nb, rowp, colp, work, mask, c0, c1, c2, f_hbm, s_hbm, g_ref, cv, fv, sv, l1, l2, sems
):
    pairs, slots, rows, tile, tile_rows, tile_cols = dims
    copies = (
        pltpu.make_async_copy(f_hbm, fv, sems.at[0]),
        pltpu.make_async_copy(s_hbm, sv, sems.at[1]),
    ) + tuple(
        pltpu.make_async_copy(c, cv.at[pl.ds(first * (pairs // 2), n * (pairs // 2))], sems.at[2 + i])
        for i, (c, (first, n)) in enumerate(zip((c0, c1, c2), SHARES))
    )
    for c in copies:
        c.start()
    row0 = lax.axis_index("row") * tile_rows
    col0 = lax.axis_index("col") * tile_cols
    g_ref[...] = jnp.zeros_like(g_ref)
    cells = tile_rows * tile_cols

    def one_pair(d, i, counts):
        p = 2 * d + i
        w = work[p]

        row, col = lax.div(d, 16), lax.rem(d, 16)
        spot = lax.rem(row, 2) * 64 + lax.div(row, 2) * 16 + col

        def busy(counts):
            out = list(counts)
            packed_rows = rowp[p]
            n_rows = w & 7
            for n in range(2):
                q = 2 * i + n
                k = nb[2 * p + n]
                packed_cols = colp[k]
                n_cols = (w >> (3 + 3 * n)) & 7

                def by_row(x, cnt, k=k, packed_cols=packed_cols, n_cols=n_cols, q=q):
                    sa = p * slots + ((packed_rows >> (3 * x)) & 7)
                    a = dom[sa] - row0
                    from_a = address[sa]

                    def by_col(y, cnt):
                        sb = k * slots + ((packed_cols >> (3 * y)) & 7)
                        b = dom[sb] - col0
                        cell = a * tile_cols + b
                        m0 = mask[cell]
                        m1 = mask[cells + cell]
                        l1[q, cnt] = from_a | (address[sb] << 11) | (a << 22) | (b << 27)
                        l2[q, cnt] = spot | (m0 << 8) | (m1 << 9)
                        return cnt + (m0 | m1)

                    return lax.fori_loop(0, n_cols, by_col, cnt)

                out[q] = lax.fori_loop(0, n_rows, by_row, out[q])
            return tuple(out)

        return lax.cond(w != 0, busy, lambda c: c, counts)

    def per_device(d, counts):
        counts = one_pair(d, 0, counts)
        return one_pair(d, 1, counts)

    zero = jnp.int32(0)
    counts = lax.fori_loop(0, pairs // 2, per_device, (zero, zero, zero, zero))
    for q in range(4):
        for x in range(UNROLL):
            l1[q, counts[q] + x] = zero
            l2[q, counts[q] + x] = zero
    for c in copies:
        c.wait()

    def product(q, i):
        w1 = l1[q, i]
        w2 = l2[q, i]
        sa = w1 & 2047
        sb = (w1 >> 11) & 2047
        a = pl.multiple_of(((w1 >> 22) & 31) * tile, tile)
        b = pl.multiple_of(((w1 >> 27) & 15) * tile, tile)
        both = jnp.concatenate([fv[pl.ds(a, tile), pl.ds(b, tile)], sv[pl.ds(a, tile), pl.ds(b, tile)]], axis=1)
        t = jnp.dot(cv[sa], both, preferred_element_type=jnp.float32)
        m0 = ((w2 >> 8) & 1).astype(jnp.float32)
        m1 = ((w2 >> 9) & 1).astype(jnp.float32)
        partner = cv[sb]
        dn = (((1,), (1,)), ((), ()))
        uf = lax.dot_general((t[:, :tile] * m0).astype(jnp.bfloat16), partner, dn, preferred_element_type=jnp.float32)
        us = lax.dot_general((t[:, tile:] * m1).astype(jnp.bfloat16), partner, dn, preferred_element_type=jnp.float32)
        return w2 & 255, uf, us

    for q in range(4):
        lo = q * LANES

        def body(it, carry, q=q, lo=lo):
            done = [product(q, it * UNROLL + x) for x in range(UNROLL)]
            for d, uf, us in done:
                g_ref[2 * d, :rows, lo : lo + rows] += uf
                g_ref[2 * d + 1, :rows, lo : lo + rows] += us
            return carry

        lax.fori_loop(0, (counts[q] + UNROLL - 1) // UNROLL, body, 0)


def shards(fock, intersection, tile_mask, coefficients, domains, neighbours, amplitudes):
    pair_dev, slots, rows, tile = coefficients.shape
    tile_rows, tile_cols = fock.shape[0] // tile, fock.shape[1] // tile
    n_dev = lax.axis_size("row") * lax.axis_size("col")
    pairs = pair_dev * n_dev
    both = ("row", "col")
    amps = jnp.pad(amplitudes.reshape(-1), (0, 7 * 128 - amplitudes.size)).reshape(7, 128)
    names = jnp.concatenate([domains.reshape(-1), neighbours.reshape(-1)]).astype(jnp.float32)
    meta = jnp.concatenate([amps, jnp.pad(names, (0, 128 - names.size)).reshape(1, 128)])
    c0, c1, c2, metas = gather_all(coefficients.reshape(pair_dev * slots, rows, tile), meta)
    metas = metas.transpose(3, 0, 1, 2, 4, 5).reshape(n_dev, 8, 128)
    ints = metas[:, 7, : names.size].astype(jnp.int32)
    dom, nb = ints[:, : domains.size].reshape(pairs, slots), ints[:, domains.size :].reshape(pairs, 2)
    rowp, rown = slot_tables(dom, lax.axis_index("row") * tile_rows, tile_rows)
    colp, coln = slot_tables(dom, lax.axis_index("col") * tile_cols, tile_cols)
    linked = jnp.take(coln, nb.reshape(-1), axis=0).reshape(pairs, 2)
    work = rown | (linked[:, 0] << 3) | (linked[:, 1] << 6)
    work = jnp.where((rown > 0) & (linked.sum(axis=1) > 0), work, 0)
    smem = pl.BlockSpec(memory_space=pltpu.SMEM)
    anys = pl.BlockSpec(memory_space=pl.ANY)
    g = pl.pallas_call(
        functools.partial(pair_blocks_kernel, (pairs, slots, rows, tile, tile_rows, tile_cols)),
        out_shape=jax.ShapeDtypeStruct((2 * n_dev, 24, 128), jnp.float32),
        name="pairs",
        in_specs=[smem] * 7 + [anys] * 5,
        out_specs=pl.BlockSpec(memory_space=pltpu.VMEM),
        scratch_shapes=[
            pltpu.VMEM((pairs * slots, rows, tile), jnp.bfloat16),
            pltpu.VMEM(fock.shape, jnp.bfloat16),
            pltpu.VMEM(fock.shape, jnp.bfloat16),
            pltpu.SMEM((4, 2048), jnp.int32),
            pltpu.SMEM((4, 2048), jnp.int32),
            pltpu.SemaphoreType.DMA((5,)),
        ],
        compiler_params=pltpu.CompilerParams(vmem_limit_bytes=56 * 2**20),
    )(
        dom.reshape(-1), jnp.asarray(slot_address(pairs, slots)), nb.reshape(-1), rowp, colp, work,
        tile_mask.reshape(-1), *(c.reshape(-1, rows, tile) for c in (c0, c1, c2)), fock, intersection,
    )
    g = reduce_all(g.reshape(2, n_dev, 24, 128))
    blocks = g[:, :rows].reshape(2, rows, 2, 2, LANES)[..., :rows]
    fock_part = jnp.transpose(blocks[0], (1, 2, 0, 3))
    over_part = jnp.transpose(blocks[1], (1, 2, 0, 3))
    picked = jnp.take(metas[:, :7], neighbours.reshape(-1) // 2, axis=0).reshape(4, -1)[:, : amplitudes.size]
    picked = picked.reshape(4, 2, rows, rows)
    odd = (neighbours.reshape(4, 1, 1) % 2) == 1
    nearby = jnp.where(odd, picked[:, 1], picked[:, 0]).reshape(2, 2, rows, rows)
    first = jnp.einsum("pnab,pnbc,pndc->pad", over_part, nearby, fock_part, precision=HIGH)
    second = jnp.einsum("pnab,pnbc,pndc->pad", fock_part, nearby, over_part, precision=HIGH)
    return first + second


def solution(mesh):
    placed = (
        P("row", "col"),
        P("row", "col"),
        P(None, "row", "col"),
        P(("row", "col"), None, None, None),
        P(("row", "col"), None),
        P(("row", "col"), None),
        P(("row", "col"), None, None),
    )
    return jax.shard_map(
        shards, mesh=mesh, in_specs=placed, out_specs=P(("row", "col"), None, None), check_vma=False
    )
```
